32 devices in a mesh: tile: 8 (over y, x, core), col: 4 (over z).
Axes of the slice: x: 2, y: 2, z: 4, core: 2. Of those that a mesh axis runs over, the one named last changes fastest.
Arguments:
- impedance: bfloat16 [2, 16384, 16384], P(None, 'tile', 'col'), may hold values from -0.0234375 to 0.0234375
- mobility: bfloat16 [256, 64, 128], P('tile'), may hold values from -0.5 to 0.5
- force: bfloat16 [512, 256, 128], P('col', 'tile'), may hold values from -6 to 6
- patch_map: int32 [16384], replicated, may hold values from 0 to 16383, each once
- ownership: int32 [256], P('tile'), may hold values from 0 to 255, each once
Outputs:
- velocity: bfloat16 [512, 256, 128], P('col', 'tile')
- pressure: bfloat16 [512, 2, 16384], P('col', None, 'tile')
The draws below stay inside these ranges and needn't reach their ends.
Inputs may be any that keep to these rules, and one draw needn't show every extreme that they name: `patch_map`: each patch appears exactly once. `ownership`: each panel appears exactly once.
All inputs are finite; a program needn't handle non-finite values.
Results may differ from the reference program's by a relative error of at most 0.018.
Values may be sent and summed in bfloat16 or wider, within the bound.
A program may use at most 128 MiB of HBM per device.

```python
import jax
import jax.numpy as jnp
from jax import lax

P_SIZE = 16384
K = 64
LOADS = 512
ITERS = 2
PANELS = 256


def level_of(own_key, extent, cuts, smallest, high):
    def one(dim, blocks):
        steps = jax.random.uniform(jax.random.fold_in(jax.random.fold_in(own_key, 6), dim), (blocks,), jnp.float32, smallest / len(cuts), high / len(cuts))
        return jnp.repeat(jnp.exp(steps), extent[dim] // blocks).reshape((-1,) + (1,) * (len(extent) - dim - 1))

    factor_of = one(*cuts[0])
    for cut in cuts[1:]:
        factor_of = factor_of * one(*cut)
    return factor_of


def centred(own_key, shape, width, most, cuts=(), held_as=jnp.bfloat16):
    level = level_of(own_key, shape, cuts, -0.22, 0.18) if cuts else 1.0
    entries = jax.random.normal(own_key, shape, jnp.float32) * width * level
    return jnp.minimum(jnp.maximum(entries, -most), most).astype(held_as)


def setup_inputs(seed: int = 0) -> dict:
    key_list = jax.random.split(jax.random.key(seed), 6)
    return {
        "impedance": centred(key_list[0], (2, P_SIZE, P_SIZE), (4 * P_SIZE) ** -0.5, 0.0234375, ((1, 8), (2, 4))),
        "mobility": centred(key_list[1], (PANELS, K, 2 * K), (2 * K) ** -0.5, 0.5, ((0, 8),)),
        "force": centred(key_list[2], (LOADS, PANELS, 2 * K), 1.0, 6.0, ((0, 4), (1, 8))),
        "patch_map": jax.random.permutation(key_list[3], P_SIZE).astype(jnp.int32),
        "ownership": jax.random.permutation(key_list[4], PANELS).astype(jnp.int32),
    }


def impedance_product(impedance, field):
    highest = lax.Precision.HIGHEST
    vel_re = field[:, 0].astype(jnp.float32)
    vel_im = field[:, 1].astype(jnp.float32)
    rows_block = P_SIZE // 16

    def one_block(block_index):
        z_block = lax.dynamic_slice_in_dim(impedance, block_index * rows_block, rows_block, 1).astype(jnp.float32)
        real_part = jnp.dot(vel_re, z_block[0].T, precision=highest) - jnp.dot(vel_im, z_block[1].T, precision=highest)
        imag_part = jnp.dot(vel_re, z_block[1].T, precision=highest) + jnp.dot(vel_im, z_block[0].T, precision=highest)
        return jnp.stack([real_part, imag_part], 1)

    blocks = lax.map(one_block, jnp.arange(16, dtype=jnp.int32))
    return jnp.transpose(blocks, (1, 2, 0, 3)).reshape(LOADS, 2, P_SIZE)


def panel_response(drive, mobility):
    highest = lax.Precision.HIGHEST
    drive_f = drive.astype(jnp.float32)
    mob_f = mobility.astype(jnp.float32)
    drive_re = drive_f[..., :K]
    drive_im = drive_f[..., K:]
    mob_re = mob_f[:, :, :K]
    mob_im = mob_f[:, :, K:]
    out_re = jnp.einsum("lsk,sjk->lsj", drive_re, mob_re, precision=highest) - jnp.einsum("lsk,sjk->lsj", drive_im, mob_im, precision=highest)
    out_im = jnp.einsum("lsk,sjk->lsj", drive_re, mob_im, precision=highest) + jnp.einsum("lsk,sjk->lsj", drive_im, mob_re, precision=highest)
    return jnp.concatenate([out_re, out_im], -1).astype(jnp.bfloat16)


def reference(impedance, mobility, force, patch_map, ownership):
    slot_patches = patch_map.reshape(P_SIZE // K, K)[ownership].reshape(P_SIZE).astype(jnp.int32)

    def to_natural(velocity_slots):
        values = velocity_slots.reshape(LOADS, P_SIZE // K, 2, K).transpose(0, 2, 1, 3).reshape(LOADS, 2, P_SIZE)
        return jnp.zeros((LOADS, 2, P_SIZE), jnp.bfloat16).at[:, :, slot_patches].set(values)

    def from_natural(field):
        return field[:, :, slot_patches].reshape(LOADS, 2, P_SIZE // K, K).transpose(0, 2, 1, 3).reshape(LOADS, P_SIZE // K, 2 * K)

    velocity = panel_response(force, mobility)
    pressure = jnp.zeros((LOADS, 2, P_SIZE), jnp.bfloat16)
    for iteration in range(ITERS):
        pressure = impedance_product(impedance, to_natural(velocity)).astype(jnp.bfloat16)
        drive = (force.astype(jnp.float32) - from_natural(pressure).astype(jnp.float32)).astype(jnp.bfloat16)
        velocity = panel_response(drive, mobility)
    return velocity, pressure
```

```python
import functools

import jax
import jax.numpy as jnp
from jax import lax
from jax.experimental import pallas as pl
from jax.experimental.pallas import tpu as pltpu
from jax.sharding import PartitionSpec as P

ITERS = 2
LANES = 128
BF16 = jnp.bfloat16
F32 = jnp.float32


def pick_kernel(index_ref, rows_ref, out_ref):
    count = out_ref.shape[0]
    step = 16

    @pl.loop(0, count // step)
    def _(block):
        base = block * step
        for k in range(step):
            out_ref[base + k] = rows_ref[index_ref[base + k]]


def pick_rows(index, rows):
    return pl.pallas_call(
        pick_kernel,
        out_shape=jax.ShapeDtypeStruct((index.shape[0],) + rows.shape[1:], rows.dtype),
        in_specs=[
            pl.BlockSpec(memory_space=pltpu.SMEM),
            pl.BlockSpec(memory_space=pltpu.VMEM),
        ],
        out_specs=pl.BlockSpec(memory_space=pltpu.VMEM),
        compiler_params=pltpu.CompilerParams(vmem_limit_bytes=40 * 2**20),
    )(index, rows)


def product_kernel(z_ref, x_ref, out_ref):
    groups, _, width = out_ref.shape
    half = width // 2
    a = jnp.dot(z_ref[0], x_ref[...], preferred_element_type=F32)
    b = jnp.dot(z_ref[1], x_ref[...], preferred_element_type=F32)
    for g in range(groups):
        re = slice(g * width, g * width + half)
        im = slice(g * width + half, (g + 1) * width)
        out_ref[g] = jnp.concatenate([a[:, re] - b[:, im], a[:, im] + b[:, re]], 1).astype(out_ref.dtype)


def product(impedance, x, groups):
    _, rows, depth = impedance.shape
    width = x.shape[1] // groups
    block = min(256, rows)
    return pl.pallas_call(
        product_kernel,
        grid=(rows // block,),
        out_shape=jax.ShapeDtypeStruct((groups, rows, width), BF16),
        in_specs=[
            pl.BlockSpec((2, block, depth), lambda i: (0, i, 0)),
            pl.BlockSpec((depth, groups * width), lambda i: (0, 0)),
        ],
        out_specs=pl.BlockSpec((groups, block, width), lambda i: (0, i, 0)),
        compiler_params=pltpu.CompilerParams(vmem_limit_bytes=48 * 2**20),
    )(impedance, x)


def inverse_permutation(sigma):
    count = sigma.shape[0]
    where = jnp.arange(count, dtype=jnp.int32)
    high = (sigma // LANES)[None, :] == jnp.arange(count // LANES, dtype=jnp.int32)[:, None]
    low = (sigma % LANES)[:, None] == jnp.arange(LANES, dtype=jnp.int32)[None, :]
    where_high = jnp.where(low, (where // LANES)[:, None], 0).astype(BF16)
    where_low = jnp.where(low, (where % LANES)[:, None], 0).astype(BF16)
    digits = jnp.dot(
        high.astype(BF16), jnp.concatenate([where_high, where_low], 1), preferred_element_type=F32
    )
    inverse = digits[:, :LANES] * LANES + digits[:, LANES:]
    return inverse.astype(jnp.int32).reshape(count)


def per_device(impedance, mobility, force, patch_map, ownership):
    slots, width, _ = mobility.shape
    patches = patch_map.shape[0]
    loads = force.shape[0]
    tiles = lax.axis_size("tile")
    cols = lax.axis_size("col")
    share = patches // cols // tiles
    mine = slots * width
    tile = lax.axis_index("tile")

    panels = patch_map.reshape(-1, width)
    slot_flat = panels[ownership].reshape(mine)
    owners = lax.all_gather(ownership, "tile", axis=0, tiled=True)
    inverse = inverse_permutation(panels[owners].reshape(patches))
    share_index = lax.dynamic_index_in_dim(
        inverse.reshape(cols, tiles, share), tile, 1, keepdims=False
    ).reshape(cols * share)

    mob_re = mobility[:, :, :width]
    mob_im = mobility[:, :, width:]
    form = jnp.stack(
        [jnp.stack([mob_re, -mob_im], -1), jnp.stack([mob_im, mob_re], -1)], 2
    ).reshape(slots, 2 * width, 2 * width)
    force_rows = force.reshape(loads, slots, 2, width).transpose(1, 3, 2, 0).reshape(slots, 2 * width, loads)

    def response(drive):
        return lax.dot_general(
            form, drive, (((2,), (1,)), ((0,), (0,))), preferred_element_type=F32
        ).astype(BF16)

    velocity = response(force_rows)
    for _ in range(ITERS):
        everyone = lax.all_gather(velocity.reshape(mine, 2, loads), "tile", axis=0, tiled=True)
        picked = pick_rows(share_index, everyone).reshape(cols, share, 2, loads)
        moved = lax.all_to_all(picked, "col", split_axis=0, concat_axis=0, tiled=True)
        columns = moved.transpose(1, 0, 2, 3).reshape(share, cols * 2 * loads)
        field = lax.all_gather(columns, "tile", axis=0, tiled=True)
        partial = product(impedance, field, cols)
        summed = lax.psum_scatter(partial, "col", scatter_dimension=0, tiled=True)
        pressure = summed.reshape(-1, 2, loads)
        gathered = lax.all_gather(pressure, "tile", axis=0, tiled=True)
        at_slots = pick_rows(slot_flat, gathered).reshape(slots, 2 * width, loads)
        drive = (force_rows.astype(F32) - at_slots.astype(F32)).astype(BF16)
        velocity = response(drive)
    velocity_out = velocity.reshape(slots, width, 2, loads).transpose(3, 0, 2, 1).reshape(loads, slots, 2 * width)
    pressure_out = pressure.transpose(2, 1, 0)
    return velocity_out, pressure_out


def solution(mesh):
    return jax.shard_map(
        per_device,
        mesh=mesh,
        in_specs=(
            P(None, "tile", "col"),
            P("tile", None, None),
            P("col", "tile", None),
            P(),
            P("tile"),
        ),
        out_specs=(P("col", "tile", None), P("col", None, "tile")),
        check_vma=False,
    )
```

```python
import functools

import jax
import jax.numpy as jnp
from jax import lax
from jax.experimental import pallas as pl
from jax.experimental.pallas import tpu as pltpu
from jax.sharding import PartitionSpec as P

ITERS = 2
LANES = 128
BF16 = jnp.bfloat16
F32 = jnp.float32


MESH = pl.DeviceIdType.MESH


def gather_over_tile(tiles, x_ref, buf, send_sem, recv_sem, own_sem, ready):
    a_size = tiles // 4
    rows = x_ref.shape[0]
    half = rows // 2
    me = lax.axis_index("tile")
    core = lax.rem(me, 2)
    my_b = lax.rem(me // 2, 2)
    my_a = me // 4
    others = range(1, a_size)

    def chip_at(oa, ob):
        return lax.rem(my_a + oa, a_size) * 2 + lax.rem(my_b + ob, 2)

    def device_at(oa, ob):
        return chip_at(oa, ob) * 2 + core

    partner = chip_at(0, 0) * 2 + 1 - core
    neighbours = [partner, device_at(0, 1)] + [device_at(o, 0) for o in others]

    barrier = pltpu.get_barrier_semaphore()
    for device in neighbours:
        pl.semaphore_signal(barrier, inc=1, device_id={"tile": device}, device_id_type=MESH)
    pl.semaphore_wait(barrier, len(neighbours))

    def piece(oa, ob, h, owner_core):
        return buf.at[chip_at(oa, ob), pl.ds(pl.multiple_of(owner_core * rows + h * half, half), half)]

    sent = []

    def send(src, dst, device, relayed, oa, ob, h):
        copy = pltpu.make_async_remote_copy(
            src_ref=src,
            dst_ref=dst,
            send_sem=send_sem.at[len(sent)],
            recv_sem=recv_sem.at[relayed, oa * 2 + ob, h],
            device_id={"tile": device},
            device_id_type=MESH,
        )
        copy.start()
        sent.append(copy)

    def arrived(relayed, oa, ob, h):
        slot = piece(oa, ob, h, 1 - core if relayed else core)
        pltpu.make_async_remote_copy(
            src_ref=slot,
            dst_ref=slot,
            send_sem=send_sem.at[0],
            recv_sem=recv_sem.at[relayed, oa * 2 + ob, h],
            device_id={"tile": partner},
            device_id_type=MESH,
        ).wait_recv()

    def relay(oa, ob, h):
        slot = piece(oa, ob, h, core)
        send(slot, slot, partner, 1, oa, ob, h)

    def forward(oa, ob, h, device, new_oa, new_ob):
        slot = piece(oa, ob, h, core)
        send(slot, slot, device, 0, new_oa, new_ob, h)

    def own(h):
        return x_ref.at[pl.ds(h * half, half)]

    for h in (1, 0):
        send(own(h), piece(0, 0, h, core), device_at(0, 1), 0, 0, 1, h)
    for h in (0, 1):
        for o in others:
            send(own(h), piece(0, 0, h, core), device_at(o, 0), 0, (a_size - o) % a_size, 0, h)
    for h in (0, 1):
        send(own(h), piece(0, 0, h, core), partner, 1, 0, 0, h)
    local = pltpu.make_async_copy(
        x_ref, buf.at[chip_at(0, 0), pl.ds(pl.multiple_of(core * rows, rows), rows)], own_sem.at[0]
    )
    local.start()
    local.wait()
    for h in (0, 1):
        arrived(1, 0, 0, h)
    ready(chip_at(0, 0))

    arrived(0, 0, 1, 1)
    for o in others:
        forward(0, 1, 1, device_at(o, 0), (a_size - o) % a_size, 1)
    for o in others:
        arrived(0, o, 0, 0)
        forward(o, 0, 0, device_at(0, 1), o, 1)
    relay(0, 1, 1)
    for o in others:
        relay(o, 0, 0)
    arrived(0, 0, 1, 0)
    relay(0, 1, 0)
    for o in others:
        arrived(0, o, 0, 1)
        relay(o, 0, 1)
    for h in (1, 0):
        arrived(1, 0, 1, h)
    ready(chip_at(0, 1))
    for o in others:
        for h in (0, 1):
            arrived(0, o, 1, h)
            relay(o, 1, h)
    for o in others:
        for h in (0, 1):
            arrived(1, o, 0, h)
        ready(chip_at(o, 0))
    for o in others:
        for h in (0, 1):
            arrived(1, o, 1, h)
        ready(chip_at(o, 1))
    for copy in sent:
        copy.wait_send()


def chip_order(tiles):
    a_size = tiles // 4
    me = lax.axis_index("tile")
    my_b = lax.rem(me // 2, 2)
    my_a = me // 4
    order = [(0, 0), (0, 1)] + [(o, b) for b in (0, 1) for o in range(1, a_size)]
    return [lax.rem(my_a + oa, a_size) * 2 + lax.rem(my_b + ob, 2) for oa, ob in order]


def gather_scratch(tiles, shape):
    a_size = tiles // 4
    copies = 2 + 2 * (a_size - 1) + 2 * (a_size - 1) + 2 * 2 * a_size
    return [
        pltpu.VMEM((tiles // 2, 2 * shape[0]) + shape[1:], BF16),
        pltpu.SemaphoreType.DMA((copies,)),
        pltpu.SemaphoreType.DMA((2, 2 * a_size, 2)),
        pltpu.SemaphoreType.DMA((1,)),
    ]


def pick_kernel(tiles, index_ref, x_ref, out_ref, buf, send_sem, recv_sem, own_sem):
    gather_over_tile(tiles, x_ref, buf, send_sem, recv_sem, own_sem, lambda chip: None)
    count = out_ref.shape[0]
    pair = buf.shape[1]
    step = 16

    @pl.loop(0, count // step)
    def _(block):
        base = block * step
        for k in range(step):
            index = index_ref[base + k]
            out_ref[base + k] = buf[index // pair, lax.rem(index, pair)]


def gather_and_pick(index, rows, tiles):
    return pl.pallas_call(
        functools.partial(pick_kernel, tiles),
        out_shape=jax.ShapeDtypeStruct((index.shape[0],) + rows.shape[1:], rows.dtype),
        in_specs=[
            pl.BlockSpec(memory_space=pltpu.SMEM),
            pl.BlockSpec(memory_space=pltpu.VMEM),
        ],
        out_specs=pl.BlockSpec(memory_space=pltpu.VMEM),
        scratch_shapes=gather_scratch(tiles, rows.shape),
        compiler_params=pltpu.CompilerParams(
            collective_id=0, has_side_effects=True, vmem_limit_bytes=40 * 2**20
        ),
    )(index, rows)


def product_kernel(tiles, z_ref, x_ref, out_ref, z_buf, z_sem, total, buf, send_sem, recv_sem, own_sem):
    groups, rows, width = out_ref.shape
    half = width // 2
    depth = z_buf.shape[3]
    block = min(256, rows)
    chips = chip_order(tiles)
    steps = len(chips)

    def fetch(step):
        start = pl.multiple_of(chips[step] * depth, depth)
        return pltpu.make_async_copy(z_ref.at[:, :, pl.ds(start, depth)], z_buf.at[step % 2], z_sem.at[step % 2])

    for step in range(min(2, steps)):
        fetch(step).start()
    done = []

    def ready(chip):
        step = len(done)
        done.append(step)
        fetch(step).wait()

        @pl.loop(0, rows // block)
        def _(i):
            at = pl.ds(pl.multiple_of(i * block, block), block)
            x = buf[chip]
            a = jnp.dot(z_buf[step % 2, 0, at, :], x, preferred_element_type=F32)
            b = jnp.dot(z_buf[step % 2, 1, at, :], x, preferred_element_type=F32)
            for g in range(groups):
                re = slice(g * width, g * width + half)
                im = slice(g * width + half, (g + 1) * width)
                term = jnp.concatenate([a[:, re] - b[:, im], a[:, im] + b[:, re]], 1)
                if step > 0:
                    term = total[g, at, :] + term
                if step < steps - 1:
                    total[g, at, :] = term
                else:
                    out_ref[g, at, :] = term.astype(out_ref.dtype)

        if step + 2 < steps:
            fetch(step + 2).start()

    gather_over_tile(tiles, x_ref, buf, send_sem, recv_sem, own_sem, ready)


def gather_and_multiply(impedance, x, groups, tiles):
    _, rows, depth = impedance.shape
    width = x.shape[1] // groups
    return pl.pallas_call(
        functools.partial(product_kernel, tiles),
        out_shape=jax.ShapeDtypeStruct((groups, rows, width), BF16),
        in_specs=[
            pl.BlockSpec(memory_space=pl.ANY),
            pl.BlockSpec(memory_space=pltpu.VMEM),
        ],
        out_specs=pl.BlockSpec(memory_space=pltpu.VMEM),
        scratch_shapes=[
            pltpu.VMEM((2, 2, rows, 2 * x.shape[0]), BF16),
            pltpu.SemaphoreType.DMA((2,)),
            pltpu.VMEM((groups, rows, width), F32),
        ]
        + gather_scratch(tiles, x.shape),
        compiler_params=pltpu.CompilerParams(
            collective_id=1, has_side_effects=True, vmem_limit_bytes=60 * 2**20
        ),
    )(impedance, x)


def inverse_permutation(sigma):
    count = sigma.shape[0]
    where = jnp.arange(count, dtype=jnp.int32)
    high = (sigma // LANES)[None, :] == jnp.arange(count // LANES, dtype=jnp.int32)[:, None]
    low = (sigma % LANES)[:, None] == jnp.arange(LANES, dtype=jnp.int32)[None, :]
    where_high = jnp.where(low, (where // LANES)[:, None], 0).astype(BF16)
    where_low = jnp.where(low, (where % LANES)[:, None], 0).astype(BF16)
    digits = jnp.dot(
        high.astype(BF16), jnp.concatenate([where_high, where_low], 1), preferred_element_type=F32
    )
    inverse = digits[:, :LANES] * LANES + digits[:, LANES:]
    return inverse.astype(jnp.int32).reshape(count)


def per_device(impedance, mobility, force, patch_map, ownership):
    slots, width, _ = mobility.shape
    patches = patch_map.shape[0]
    loads = force.shape[0]
    tiles = lax.axis_size("tile")
    cols = lax.axis_size("col")
    share = patches // cols // tiles
    mine = slots * width
    tile = lax.axis_index("tile")

    panels = patch_map.reshape(-1, width)
    slot_flat = panels[ownership].reshape(mine)
    owners = lax.all_gather(ownership, "tile", axis=0, tiled=True)
    inverse = inverse_permutation(panels[owners].reshape(patches))
    share_index = lax.dynamic_index_in_dim(
        inverse.reshape(cols, tiles, share), tile, 1, keepdims=False
    ).reshape(cols * share)

    mob_re = mobility[:, :, :width]
    mob_im = mobility[:, :, width:]
    form = jnp.stack(
        [jnp.stack([mob_re, -mob_im], -1), jnp.stack([mob_im, mob_re], -1)], 2
    ).reshape(slots, 2 * width, 2 * width)
    force_rows = force.reshape(loads, slots, 2, width).transpose(1, 3, 2, 0).reshape(slots, 2 * width, loads)

    def response(drive):
        return lax.dot_general(
            form, drive, (((2,), (1,)), ((0,), (0,))), preferred_element_type=F32
        ).astype(BF16)

    velocity = response(force_rows)
    for _ in range(ITERS):
        picked = gather_and_pick(share_index, velocity.reshape(mine, 2, loads), tiles)
        picked = picked.reshape(cols, share, 2, loads)
        moved = lax.all_to_all(picked, "col", split_axis=0, concat_axis=0, tiled=True)
        columns = moved.transpose(1, 0, 2, 3).reshape(share, cols * 2 * loads)
        partial = gather_and_multiply(impedance, columns, cols, tiles)
        summed = lax.psum_scatter(partial, "col", scatter_dimension=0, tiled=True)
        pressure = summed.reshape(-1, 2, loads)
        at_slots = gather_and_pick(slot_flat, pressure, tiles).reshape(slots, 2 * width, loads)
        drive = (force_rows.astype(F32) - at_slots.astype(F32)).astype(BF16)
        velocity = response(drive)
    velocity_out = velocity.reshape(slots, width, 2, loads).transpose(3, 0, 2, 1).reshape(loads, slots, 2 * width)
    pressure_out = pressure.transpose(2, 1, 0)
    return velocity_out, pressure_out


def solution(mesh):
    return jax.shard_map(
        per_device,
        mesh=mesh,
        in_specs=(
            P(None, "tile", "col"),
            P("tile", None, None),
            P("col", "tile", None),
            P(),
            P("tile"),
        ),
        out_specs=(P("col", "tile", None), P("col", None, "tile")),
        check_vma=False,
    )
```

```python
import functools

import jax
import jax.numpy as jnp
from jax import lax
from jax.experimental import pallas as pl
from jax.experimental.pallas import tpu as pltpu
from jax.sharding import PartitionSpec as P

ITERS = 2
LANES = 128
BF16 = jnp.bfloat16
F32 = jnp.float32


MESH = pl.DeviceIdType.MESH


def gather_over_tile(tiles, x_ref, buf, send_sem, recv_sem, own_sem, ready):
    a_size = tiles // 4
    rows = x_ref.shape[0]
    half = rows // 2
    me = lax.axis_index("tile")
    core = lax.rem(me, 2)
    my_b = lax.rem(me // 2, 2)
    my_a = me // 4
    others = range(1, a_size)

    def chip_at(oa, ob):
        return lax.rem(my_a + oa, a_size) * 2 + lax.rem(my_b + ob, 2)

    def device_at(oa, ob):
        return chip_at(oa, ob) * 2 + core

    partner = chip_at(0, 0) * 2 + 1 - core
    neighbours = [partner, device_at(0, 1)] + [device_at(o, 0) for o in others]

    barrier = pltpu.get_barrier_semaphore()
    for device in neighbours:
        pl.semaphore_signal(barrier, inc=1, device_id={"tile": device}, device_id_type=MESH)
    pl.semaphore_wait(barrier, len(neighbours))

    def piece(oa, ob, h, owner_core):
        return buf.at[chip_at(oa, ob), pl.ds(pl.multiple_of(owner_core * rows + h * half, half), half)]

    sent = []

    def send(src, dst, device, relayed, oa, ob, h):
        copy = pltpu.make_async_remote_copy(
            src_ref=src,
            dst_ref=dst,
            send_sem=send_sem.at[len(sent)],
            recv_sem=recv_sem.at[relayed, oa * 2 + ob, h],
            device_id={"tile": device},
            device_id_type=MESH,
        )
        copy.start()
        sent.append(copy)

    def arrived(relayed, oa, ob, h):
        slot = piece(oa, ob, h, 1 - core if relayed else core)
        pltpu.make_async_remote_copy(
            src_ref=slot,
            dst_ref=slot,
            send_sem=send_sem.at[0],
            recv_sem=recv_sem.at[relayed, oa * 2 + ob, h],
            device_id={"tile": partner},
            device_id_type=MESH,
        ).wait_recv()

    def relay(oa, ob, h):
        slot = piece(oa, ob, h, core)
        send(slot, slot, partner, 1, oa, ob, h)

    def forward(oa, ob, h, device, new_oa, new_ob):
        slot = piece(oa, ob, h, core)
        send(slot, slot, device, 0, new_oa, new_ob, h)

    def own(h):
        return x_ref.at[pl.ds(h * half, half)]

    for h in (0, 1):
        send(own(h), piece(0, 0, h, core), partner, 1, 0, 0, h)
    for h in (1, 0):
        send(own(h), piece(0, 0, h, core), device_at(0, 1), 0, 0, 1, h)
    for h in (0, 1):
        for o in others:
            send(own(h), piece(0, 0, h, core), device_at(o, 0), 0, (a_size - o) % a_size, 0, h)
    local = pltpu.make_async_copy(
        x_ref, buf.at[chip_at(0, 0), pl.ds(pl.multiple_of(core * rows, rows), rows)], own_sem.at[0]
    )
    local.start()
    local.wait()
    for h in (0, 1):
        arrived(1, 0, 0, h)
    ready(chip_at(0, 0))

    arrived(0, 0, 1, 1)
    for o in others:
        forward(0, 1, 1, device_at(o, 0), (a_size - o) % a_size, 1)
    for o in others:
        arrived(0, o, 0, 0)
        forward(o, 0, 0, device_at(0, 1), o, 1)
    relay(0, 1, 1)
    for o in others:
        relay(o, 0, 0)
    arrived(0, 0, 1, 0)
    relay(0, 1, 0)
    for o in others:
        arrived(0, o, 0, 1)
        relay(o, 0, 1)
    for h in (1, 0):
        arrived(1, 0, 1, h)
    ready(chip_at(0, 1))
    for o in others:
        for h in (0, 1):
            arrived(0, o, 1, h)
            relay(o, 1, h)
    for o in others:
        for h in (0, 1):
            arrived(1, o, 0, h)
        ready(chip_at(o, 0))
    for o in others:
        for h in (0, 1):
            arrived(1, o, 1, h)
        ready(chip_at(o, 1))
    for copy in sent:
        copy.wait_send()


def chip_order(tiles):
    a_size = tiles // 4
    me = lax.axis_index("tile")
    my_b = lax.rem(me // 2, 2)
    my_a = me // 4
    order = [(0, 0), (0, 1)] + [(o, b) for b in (0, 1) for o in range(1, a_size)]
    return [lax.rem(my_a + oa, a_size) * 2 + lax.rem(my_b + ob, 2) for oa, ob in order]


def gather_scratch(tiles, shape):
    a_size = tiles // 4
    copies = 2 + 2 * (a_size - 1) + 2 * (a_size - 1) + 2 * 2 * a_size
    return [
        pltpu.VMEM((tiles // 2, 2 * shape[0]) + shape[1:], BF16),
        pltpu.SemaphoreType.DMA((copies,)),
        pltpu.SemaphoreType.DMA((2, 2 * a_size, 2)),
        pltpu.SemaphoreType.DMA((1,)),
    ]


def pick_kernel(tiles, index_ref, x_ref, out_ref, buf, send_sem, recv_sem, own_sem):
    gather_over_tile(tiles, x_ref, buf, send_sem, recv_sem, own_sem, lambda chip: None)
    count = out_ref.shape[0]
    pair = buf.shape[1]
    step = 16

    @pl.loop(0, count // step)
    def _(block):
        base = block * step
        for k in range(step):
            index = index_ref[base + k]
            out_ref[base + k] = buf[index // pair, lax.rem(index, pair)]


def gather_and_pick(index, rows, tiles):
    return pl.pallas_call(
        functools.partial(pick_kernel, tiles),
        out_shape=jax.ShapeDtypeStruct((index.shape[0],) + rows.shape[1:], rows.dtype),
        in_specs=[
            pl.BlockSpec(memory_space=pltpu.SMEM),
            pl.BlockSpec(memory_space=pltpu.VMEM),
        ],
        out_specs=pl.BlockSpec(memory_space=pltpu.VMEM),
        scratch_shapes=gather_scratch(tiles, rows.shape),
        compiler_params=pltpu.CompilerParams(
            collective_id=0, has_side_effects=True, vmem_limit_bytes=40 * 2**20
        ),
    )(index, rows)


def product_kernel(tiles, z_ref, x_ref, out_ref, z_buf, z_sem, total, buf, send_sem, recv_sem, own_sem):
    groups, rows, width = out_ref.shape
    half = width // 2
    depth = z_buf.shape[3]
    block = min(256, rows)
    chips = chip_order(tiles)
    steps = len(chips)

    def fetch(step):
        start = pl.multiple_of(chips[step] * depth, depth)
        return pltpu.make_async_copy(z_ref.at[:, :, pl.ds(start, depth)], z_buf.at[step % 2], z_sem.at[step % 2])

    for step in range(min(2, steps)):
        fetch(step).start()
    done = []

    def ready(chip):
        step = len(done)
        done.append(step)
        fetch(step).wait()

        @pl.loop(0, rows // block)
        def _(i):
            at = pl.ds(pl.multiple_of(i * block, block), block)
            x = buf[chip]
            a = jnp.dot(z_buf[step % 2, 0, at, :], x, preferred_element_type=F32)
            b = jnp.dot(z_buf[step % 2, 1, at, :], x, preferred_element_type=F32)
            for g in range(groups):
                re = slice(g * width, g * width + half)
                im = slice(g * width + half, (g + 1) * width)
                term = jnp.concatenate([a[:, re] - b[:, im], a[:, im] + b[:, re]], 1)
                if step > 0:
                    term = total[g, at, :] + term
                if step < steps - 1:
                    total[g, at, :] = term
                else:
                    out_ref[g, at, :] = term.astype(out_ref.dtype)

        if step + 2 < steps:
            fetch(step + 2).start()

    gather_over_tile(tiles, x_ref, buf, send_sem, recv_sem, own_sem, ready)


def gather_and_multiply(impedance, x, groups, tiles):
    _, rows, depth = impedance.shape
    width = x.shape[1] // groups
    return pl.pallas_call(
        functools.partial(product_kernel, tiles),
        out_shape=jax.ShapeDtypeStruct((groups, rows, width), BF16),
        in_specs=[
            pl.BlockSpec(memory_space=pl.ANY),
            pl.BlockSpec(memory_space=pltpu.VMEM),
        ],
        out_specs=pl.BlockSpec(memory_space=pltpu.VMEM),
        scratch_shapes=[
            pltpu.VMEM((2, 2, rows, 2 * x.shape[0]), BF16),
            pltpu.SemaphoreType.DMA((2,)),
            pltpu.VMEM((groups, rows, width), F32),
        ]
        + gather_scratch(tiles, x.shape),
        compiler_params=pltpu.CompilerParams(
            collective_id=1, has_side_effects=True, vmem_limit_bytes=60 * 2**20
        ),
    )(impedance, x)


def inverse_permutation(sigma):
    count = sigma.shape[0]
    where = jnp.arange(count, dtype=jnp.int32)
    high = (sigma // LANES)[None, :] == jnp.arange(count // LANES, dtype=jnp.int32)[:, None]
    low = (sigma % LANES)[:, None] == jnp.arange(LANES, dtype=jnp.int32)[None, :]
    where_high = jnp.where(low, (where // LANES)[:, None], 0).astype(BF16)
    where_low = jnp.where(low, (where % LANES)[:, None], 0).astype(BF16)
    digits = jnp.dot(
        high.astype(BF16), jnp.concatenate([where_high, where_low], 1), preferred_element_type=F32
    )
    inverse = digits[:, :LANES] * LANES + digits[:, LANES:]
    return inverse.astype(jnp.int32).reshape(count)


def per_device(impedance, mobility, force, patch_map, ownership):
    slots, width, _ = mobility.shape
    patches = patch_map.shape[0]
    loads = force.shape[0]
    tiles = lax.axis_size("tile")
    cols = lax.axis_size("col")
    share = patches // cols // tiles
    mine = slots * width
    tile = lax.axis_index("tile")

    panels = patch_map.reshape(-1, width)
    slot_flat = panels[ownership].reshape(mine)
    owners = lax.all_gather(ownership, "tile", axis=0, tiled=True)
    inverse = inverse_permutation(panels[owners].reshape(patches))
    share_index = lax.dynamic_index_in_dim(
        inverse.reshape(cols, tiles, share), tile, 1, keepdims=False
    ).reshape(cols * share)

    mob_re = mobility[:, :, :width]
    mob_im = mobility[:, :, width:]
    form = jnp.stack(
        [jnp.stack([mob_re, -mob_im], -1), jnp.stack([mob_im, mob_re], -1)], 2
    ).reshape(slots, 2 * width, 2 * width)
    force_rows = force.reshape(loads, slots, 2, width).transpose(1, 3, 2, 0).reshape(slots, 2 * width, loads)

    def response(drive):
        return lax.dot_general(
            form, drive, (((2,), (1,)), ((0,), (0,))), preferred_element_type=F32
        ).astype(BF16)

    velocity = response(force_rows)
    for _ in range(ITERS):
        picked = gather_and_pick(share_index, velocity.reshape(mine, 2, loads), tiles)
        picked = picked.reshape(cols, share, 2, loads)
        moved = lax.all_to_all(picked, "col", split_axis=0, concat_axis=0, tiled=True)
        columns = moved.transpose(1, 0, 2, 3).reshape(share, cols * 2 * loads)
        partial = gather_and_multiply(impedance, columns, cols, tiles)
        summed = lax.psum_scatter(partial, "col", scatter_dimension=0, tiled=True)
        pressure = summed.reshape(-1, 2, loads)
        at_slots = gather_and_pick(slot_flat, pressure, tiles).reshape(slots, 2 * width, loads)
        drive = (force_rows.astype(F32) - at_slots.astype(F32)).astype(BF16)
        velocity = response(drive)
    velocity_out = velocity.reshape(slots, width, 2, loads).transpose(3, 0, 2, 1).reshape(loads, slots, 2 * width)
    pressure_out = pressure.transpose(2, 1, 0)
    return velocity_out, pressure_out


def solution(mesh):
    return jax.shard_map(
        per_device,
        mesh=mesh,
        in_specs=(
            P(None, "tile", "col"),
            P("tile", None, None),
            P("col", "tile", None),
            P(),
            P("tile"),
        ),
        out_specs=(P("col", "tile", None), P("col", None, "tile")),
        check_vma=False,
    )
```
